32 devices in a mesh: grp: 4 (over z), aux: 8 (over y, x, core).
Axes of the slice: x: 2, y: 2, z: 4, core: 2. Of those that a mesh axis runs over, the one named last changes fastest.
Arguments:
- integrals: bfloat16 [2048, 16384], P('aux', 'grp'), parts along dimension 1, may hold values from -6 to 6
- inverses: bfloat16 [4, 512, 512], P(None, 'aux'), as said below
- lower_blocks: bfloat16 [6, 512, 512], P(None, 'aux'), may hold values from -0.25 to 0.25
Outputs:
- solved: bfloat16 [2048, 16384], P(None, ('grp', 'aux')), parts along dimension 1
The draws below stay inside these ranges and needn't reach their ends.
There are 4 independent parts, one for each index of `grp`. The reference program is written for one: setup_inputs(seed, part) draws one part's arguments, and reference() takes and returns one part's arrays. A program takes and returns all parts, laid end to end along the dimension named above; an argument that names none is the same for every part. Nothing has to cross between parts.
Inputs may be any that keep to these rules, and one draw needn't show every extreme that they name: Each inverses[k] is lower triangular with diagonal entries between 0.5 and 1.5.
All inputs are finite; a program needn't handle non-finite values.
Results may differ from the reference program's by a relative error of at most 0.007.
Values may be sent and summed in bfloat16 or wider, within the bound.
A program may use at most 64 MiB of HBM per device.

```python
import jax
import jax.numpy as jnp

PANEL = 512
PANELS = 4
NAUXW = 2048
NBLOCKS = 6
ROWS = 4096


def draw_inverses(key, part):
    key_off = jax.random.fold_in(key, 11)
    key_diag = jax.random.fold_in(key, 12)
    shape = (PANELS, PANEL, PANEL)
    offdiag = jax.random.normal(key_off, shape, jnp.float32) * (1.5 * PANEL ** (-0.5))
    diag_vals = jax.random.uniform(key_diag, shape, jnp.float32, 0.5, 1.5)
    row_ids = jax.lax.broadcasted_iota(jnp.int32, shape, 1)
    col_ids = jax.lax.broadcasted_iota(jnp.int32, shape, 2)
    result = jnp.where(row_ids > col_ids, offdiag, 0.0) + jnp.where(row_ids == col_ids, diag_vals, 0.0)
    return result.astype(jnp.bfloat16)


def levels(own_key, shape, split, least, high):
    def one(axis_at, blocks):
        steps = jax.random.uniform(jax.random.fold_in(jax.random.fold_in(own_key, 6), axis_at), (blocks,), jnp.float32, least / len(split), high / len(split))
        return jnp.repeat(jnp.exp(steps), shape[axis_at] // blocks).reshape((-1,) + (1,) * (len(shape) - axis_at - 1))

    level = one(*split[0])
    for cut in split[1:]:
        level = level * one(*cut)
    return level


def bell_draw(own_key, dims, spread, most, shards=(), kind=jnp.bfloat16):
    drawn = spread * jax.random.normal(own_key, dims, jnp.float32)
    if shards:
        drawn = drawn * levels(own_key, dims, shards, -0.22, 0.18)
    return jnp.clip(drawn, -most, most).astype(kind)


def setup_inputs(seed: int = 0, part: int = 0) -> dict:
    key_list = jax.random.split(jax.random.key(seed), 4)
    part_splits = jax.random.split(jax.random.fold_in(key_list[3], part), 4)
    return {
        "integrals": bell_draw(part_splits[0], (NAUXW, ROWS), 1.0, 6.0, ((0, 8),)),
        "inverses": draw_inverses(jax.random.fold_in(key_list[3], 71), part),
        "lower_blocks": bell_draw(key_list[2], (NBLOCKS, PANEL, PANEL), PANEL ** -0.5, 0.25, ((1, 8),)),
    }


def reference(integrals, inverses, lower_blocks):
    outs = []
    for k in range(PANELS):
        acc = integrals[k * PANEL:(k + 1) * PANEL, :].astype(jnp.float32)
        for j in range(k):
            acc = acc - jnp.dot(lower_blocks[k * (k - 1) // 2 + j], outs[j], preferred_element_type=jnp.float32)
        rest = acc.astype(jnp.bfloat16)
        outs.append(jnp.dot(inverses[k], rest, preferred_element_type=jnp.float32).astype(jnp.bfloat16))
    return jnp.concatenate(outs, axis=0)
```

```python
import functools

import jax
import jax.numpy as jnp
from jax import lax
from jax.experimental import pallas as pl
from jax.experimental.pallas import tpu as pltpu
from jax.sharding import PartitionSpec as P

MESH = pl.DeviceIdType.MESH
PARTS = 2


def flip(index, offset):
    result = 0
    bit = 1
    while bit <= offset or bit == 1:
        if offset & bit:
            result = result + bit * ((index // bit + 1) % 2)
        else:
            result = result + bit * ((index // bit) % 2)
        bit *= 2
    return result + (index // bit) * bit


def kernel(n, pair, x_ref, inv_ref, low_ref, out_ref, cols, inv_all, low_all,
           a2a_send, a2a_recv, fac_send, fac_recv, own_send, own_recv, local_sem):
    me = lax.axis_index("aux")
    group = lax.axis_index("grp")
    held = x_ref.shape[0]
    width = out_ref.shape[1]
    part = width // PARTS
    count, rows, panel = inv_ref.shape
    mate = flip(me, 1)
    halves = 2 if pair else 1
    half = group % 2 if pair else 0
    other = (group + 1) % 2
    twin = flip(group, 1)

    def at(device):
        return pl.ds(pl.multiple_of(device * rows, rows), rows)

    locals_ = []
    mine = pl.ds(pl.multiple_of(me * held, held), held)
    for h in range(PARTS):
        locals_.append(pltpu.make_async_copy(
            x_ref.at[:, pl.ds(pl.multiple_of(me * width + h * part, part), part)],
            cols.at[mine, pl.ds(h * part, part)],
            local_sem.at[h]))
    locals_.append(pltpu.make_async_copy(inv_ref, inv_all.at[:, at(me)], local_sem.at[PARTS]))
    locals_.append(pltpu.make_async_copy(low_ref, low_all.at[:, at(me)], local_sem.at[PARTS + 1]))
    for copy in locals_:
        copy.start()

    barrier = pltpu.get_barrier_semaphore()
    for o in range(1, n):
        pl.semaphore_signal(barrier, inc=1, device_id={"aux": flip(me, o)}, device_id_type=MESH)
    if pair:
        pl.semaphore_signal(barrier, inc=1, device_id={"grp": twin}, device_id_type=MESH)
    pl.semaphore_wait(barrier, n if pair else n - 1)

    steps = [o for o in range(2, n, 2)]

    def blocks(ref, which):
        size = ref.shape[0] // halves
        return pl.ds(which * size, size)

    def factor(kind, slot, which, owner, target, first=False):
        copies = []
        for i, (src, dst) in enumerate(((inv_ref, inv_all), (low_ref, low_all))):
            place = dst.at[blocks(dst, which), at(owner)]
            copies.append(pltpu.make_async_remote_copy(
                src_ref=src.at[blocks(src, which)] if first else place,
                dst_ref=place,
                send_sem=fac_send.at[kind, slot, i],
                recv_sem=fac_recv.at[kind, slot, i],
                device_id=target,
                device_id_type=MESH))
        return copies

    def start(copies):
        for copy in copies:
            copy.start()
        return copies

    pending = []
    gather = [start(factor(0, s, half, me, {"aux": flip(me, o)}, True)) for s, o in enumerate(steps)]
    own = []
    for i, (src, dst) in enumerate(((inv_ref, inv_all), (low_ref, low_all))):
        own.append(pltpu.make_async_remote_copy(
            src_ref=src, dst_ref=dst.at[:, at(me)],
            send_sem=own_send.at[i], recv_sem=own_recv.at[i],
            device_id={"aux": mate}, device_id_type=MESH))
    start(own)

    order = sorted(range(1, n), key=lambda o: (-(o % 2 == 0), -o))
    order = [o for o in order if o != 1] + [1]
    moves = []
    for h in range(PARTS):
        group_moves = []
        for o in order:
            peer = flip(me, o)
            group_moves.append(pltpu.make_async_remote_copy(
                src_ref=x_ref.at[:, pl.ds(pl.multiple_of(peer * width + h * part, part), part)],
                dst_ref=cols.at[mine, pl.ds(h * part, part)],
                send_sem=a2a_send.at[h, o],
                recv_sem=a2a_recv.at[h, o],
                device_id={"aux": peer}, device_id_type=MESH))
        moves.append(start(group_moves))

    for s, o in enumerate(steps):
        for copy in gather[s]:
            copy.wait_recv()
        owner = flip(me, o)
        if pair:
            pending.append(start(factor(1, s, half, owner, {"grp": twin})))
        pending.append(start(factor(2, s, half, owner, {"aux": mate})))
    if pair:
        for s, o in enumerate(steps):
            for copy in factor(1, s, other, flip(me, o), {"grp": twin}):
                copy.wait_recv()
            pending.append(start(factor(3, s, other, flip(me, o), {"aux": mate})))
    for s, o in enumerate(steps):
        for copy in factor(2, s, half, flip(mate, o), {"aux": mate}):
            copy.wait_recv()
        if pair:
            for copy in factor(3, s, other, flip(mate, o), {"aux": mate}):
                copy.wait_recv()
    for copy in own:
        copy.wait_recv()
    for copy in locals_[PARTS:]:
        copy.wait()

    for h in range(PARTS):
        locals_[h].wait()
        for copy in moves[h]:
            copy.wait_recv()
        here = pl.ds(h * part, part)
        for k in range(count):
            acc = cols[pl.ds(k * panel, panel), here].astype(jnp.float32)
            for j in range(k):
                acc = acc - jnp.dot(
                    low_all[k * (k - 1) // 2 + j],
                    out_ref[pl.ds(j * panel, panel), here],
                    preferred_element_type=jnp.float32)
            rest = acc.astype(jnp.bfloat16)
            out_ref[pl.ds(k * panel, panel), here] = jnp.dot(
                inv_all[k], rest, preferred_element_type=jnp.float32).astype(jnp.bfloat16)

    for copies in gather + [own] + moves + pending:
        for copy in copies:
            copy.wait_send()


def local(n, groups, integrals, inverses, lower_blocks):
    count, rows, panel = inverses.shape
    blocks = lower_blocks.shape[0]
    held = integrals.shape[0]
    width = integrals.shape[1] // n
    pair = groups % 2 == 0 and count % 2 == 0 and blocks % 2 == 0
    slots = max(n // 2 - 1, 1)
    return pl.pallas_call(
        functools.partial(kernel, n, pair),
        out_shape=jax.ShapeDtypeStruct((held * n, width), jnp.bfloat16),
        in_specs=[pl.BlockSpec(memory_space=pltpu.HBM)] * 3,
        out_specs=pl.BlockSpec(memory_space=pltpu.VMEM),
        scratch_shapes=[
            pltpu.VMEM((held * n, width), jnp.bfloat16),
            pltpu.VMEM((count, rows * n, panel), jnp.bfloat16),
            pltpu.VMEM((blocks, rows * n, panel), jnp.bfloat16),
            pltpu.SemaphoreType.DMA((PARTS, n)),
            pltpu.SemaphoreType.DMA((PARTS, n)),
            pltpu.SemaphoreType.DMA((4, slots, 2)),
            pltpu.SemaphoreType.DMA((4, slots, 2)),
            pltpu.SemaphoreType.DMA((2,)),
            pltpu.SemaphoreType.DMA((2,)),
            pltpu.SemaphoreType.DMA((PARTS + 2,)),
        ],
        compiler_params=pltpu.CompilerParams(collective_id=0, has_side_effects=True),
    )(integrals, inverses, lower_blocks)


def solution(mesh):
    placed = (P("aux", "grp"), P(None, "aux", None), P(None, "aux", None))
    body = functools.partial(local, mesh.shape["aux"], mesh.shape["grp"])
    return jax.shard_map(
        body, mesh=mesh, in_specs=placed, out_specs=P(None, ("grp", "aux")), check_vma=False
    )
```

```python
import functools

import jax
import jax.numpy as jnp
from jax import lax
from jax.experimental import pallas as pl
from jax.experimental.pallas import tpu as pltpu
from jax.sharding import PartitionSpec as P

MESH = pl.DeviceIdType.MESH
PARTS = 2


def flip(index, offset):
    result = 0
    bit = 1
    while bit <= offset or bit == 1:
        if offset & bit:
            result = result + bit * ((index // bit + 1) % 2)
        else:
            result = result + bit * ((index // bit) % 2)
        bit *= 2
    return result + (index // bit) * bit


def kernel(n, pair, colors, x_ref, inv_ref, low_ref, out_ref, cols, fac,
           a2a_send, a2a_recv, fac_send, fac_recv, own_send, own_recv, local_sem, fac_sem):
    me = lax.axis_index("aux")
    group = lax.axis_index("grp")
    held = x_ref.shape[0]
    width = out_ref.shape[1]
    part = width // PARTS
    count, rows, panel = inv_ref.shape
    total = fac.shape[0]
    slab = rows // colors
    mate = flip(me, 1)
    size = total // 2 if pair else total
    half = group % 2 if pair else 0
    other = (group + 1) % 2
    twin = flip(group, 1)

    def low_at(k, j):
        return k * (k + 1) // 2 + j

    def inv_at(k):
        return k * (k + 1) // 2 + k

    def at(device, color=None):
        if color is None:
            return pl.ds(pl.multiple_of(device * rows, rows), rows)
        return pl.ds(pl.multiple_of(device * rows + color * slab, slab), slab)

    fill = []
    for k in range(count):
        for j in range(k):
            fill.append((low_ref.at[k * (k - 1) // 2 + j], low_at(k, j)))
        fill.append((inv_ref.at[k], inv_at(k)))
    fill = [pltpu.make_async_copy(src, fac.at[i, at(me)], fac_sem.at[i]) for src, i in fill]
    for copy in fill:
        copy.start()
    mine = pl.ds(pl.multiple_of(me * held, held), held)
    locals_ = []
    for h in range(PARTS):
        locals_.append(pltpu.make_async_copy(
            x_ref.at[:, pl.ds(pl.multiple_of(me * width + h * part, part), part)],
            cols.at[mine, pl.ds(h * part, part)],
            local_sem.at[h]))
        locals_[h].start()

    barrier = pltpu.get_barrier_semaphore()
    for o in range(1, n):
        pl.semaphore_signal(barrier, inc=1, device_id={"aux": flip(me, o)}, device_id_type=MESH)
    if pair:
        pl.semaphore_signal(barrier, inc=1, device_id={"grp": twin}, device_id_type=MESH)
    for copy in fill:
        copy.wait()
    pl.semaphore_wait(barrier, n if pair else n - 1)

    def piece(kind, color, offset, which, owner, target):
        place = fac.at[pl.ds(which * size, size), at(owner, color)]
        return pltpu.make_async_remote_copy(
            src_ref=place, dst_ref=place,
            send_sem=fac_send.at[kind, color, offset // 2],
            recv_sem=fac_recv.at[kind, color, offset // 2],
            device_id=target, device_id_type=MESH)

    bits = [2 ** i for i in range(1, n.bit_length() - 1)]
    first, relays = [], []
    for step in range(len(bits)):
        for color in range(colors):
            order = bits if color == 0 else bits[::-1]
            first.append((color, 0, order[step]))
            reached = [0]
            for bit in order[:step]:
                reached += [o + bit for o in reached]
            relays += [(color, o, order[step]) for o in reached if o]

    started = []

    def start(copy):
        copy.start()
        started.append(copy)

    def send(color, offset, bit):
        start(piece(0, color, offset ^ bit, half, flip(me, offset), {"aux": flip(me, bit)}))

    for hop in first:
        send(*hop)
    own = pltpu.make_async_remote_copy(
        src_ref=fac.at[:, at(me)], dst_ref=fac.at[:, at(me)],
        send_sem=own_send.at[0], recv_sem=own_recv.at[0],
        device_id={"aux": mate}, device_id_type=MESH)
    start(own)

    seen = []

    def arrived(color, offset):
        if (color, offset) in seen:
            return
        seen.append((color, offset))
        owner = flip(me, offset)
        piece(0, color, offset, half, owner, {"aux": mate}).wait_recv()
        for c, o, bit in relays:
            if (c, o) == (color, offset):
                send(c, o, bit)
        if pair:
            start(piece(1, color, offset, half, owner, {"grp": twin}))
        start(piece(2, color, offset, half, owner, {"aux": mate}))

    for color, offset, _ in relays:
        arrived(color, offset)

    order = [o for o in range(n - 1, 0, -1)]
    order = [o for o in order if o % 2 == 0] + [o for o in order if o % 2]
    moves = []
    for h in range(PARTS):
        moves.append([])
        for o in order:
            peer = flip(me, o)
            copy = pltpu.make_async_remote_copy(
                src_ref=x_ref.at[:, pl.ds(pl.multiple_of(peer * width + h * part, part), part)],
                dst_ref=cols.at[mine, pl.ds(h * part, part)],
                send_sem=a2a_send.at[h, o],
                recv_sem=a2a_recv.at[h, o],
                device_id={"aux": peer}, device_id_type=MESH)
            moves[h].append(copy)
            start(copy)

    for color, offset, bit in first + relays:
        arrived(color, offset ^ bit)
    if pair:
        for color, offset in seen:
            owner = flip(me, offset)
            piece(1, color, offset, other, owner, {"grp": twin}).wait_recv()
            start(piece(3, color, offset, other, owner, {"aux": mate}))
    for color, offset in seen:
        owner = flip(mate, offset)
        piece(2, color, offset, half, owner, {"aux": mate}).wait_recv()
        if pair:
            piece(3, color, offset, other, owner, {"aux": mate}).wait_recv()
    own.wait_recv()

    for h in range(PARTS):
        locals_[h].wait()
        for copy in moves[h]:
            copy.wait_recv()
        here = pl.ds(h * part, part)
        for k in range(count):
            acc = cols[pl.ds(k * panel, panel), here].astype(jnp.float32)
            for j in range(k):
                acc = acc - jnp.dot(
                    fac[low_at(k, j)], out_ref[pl.ds(j * panel, panel), here],
                    preferred_element_type=jnp.float32)
            rest = acc.astype(jnp.bfloat16)
            out_ref[pl.ds(k * panel, panel), here] = jnp.dot(
                fac[inv_at(k)], rest, preferred_element_type=jnp.float32).astype(jnp.bfloat16)

    for copy in started:
        copy.wait_send()


def local(n, groups, integrals, inverses, lower_blocks):
    count, rows, panel = inverses.shape
    blocks = count + lower_blocks.shape[0]
    held = integrals.shape[0]
    width = integrals.shape[1] // n
    pair = groups % 2 == 0 and blocks % 2 == 0
    colors = 2 if rows % 32 == 0 else 1
    slots = max(n // 2, 1)
    return pl.pallas_call(
        functools.partial(kernel, n, pair, colors),
        out_shape=pltpu.VMEM((held * n, width), jnp.bfloat16),
        in_specs=[pl.BlockSpec(memory_space=pltpu.HBM)] * 3,
        out_specs=pl.BlockSpec(memory_space=pltpu.VMEM),
        scratch_shapes=[
            pltpu.VMEM((held * n, width), jnp.bfloat16),
            pltpu.VMEM((blocks, rows * n, panel), jnp.bfloat16),
            pltpu.SemaphoreType.DMA((PARTS, n)),
            pltpu.SemaphoreType.DMA((PARTS, n)),
            pltpu.SemaphoreType.DMA((4, colors, slots)),
            pltpu.SemaphoreType.DMA((4, colors, slots)),
            pltpu.SemaphoreType.DMA((1,)),
            pltpu.SemaphoreType.DMA((1,)),
            pltpu.SemaphoreType.DMA((PARTS,)),
            pltpu.SemaphoreType.DMA((blocks,)),
        ],
        compiler_params=pltpu.CompilerParams(
            collective_id=0, has_side_effects=True, vmem_limit_bytes=32 * 2**20),
    )(*(pltpu.with_memory_space_constraint(a, pltpu.HBM) for a in (integrals, inverses, lower_blocks)))


def solution(mesh):
    placed = (P("aux", "grp"), P(None, "aux", None), P(None, "aux", None))
    body = functools.partial(local, mesh.shape["aux"], mesh.shape["grp"])
    return jax.shard_map(
        body, mesh=mesh, in_specs=placed, out_specs=P(None, ("grp", "aux")), check_vma=False
    )
```
